256 devices in a mesh: client: 128 (over y, z, x), param: 2 (over core).
Axes of the slice: x: 4, y: 4, z: 8, core: 2. Of those that a mesh axis runs over, the one named last changes fastest.
Arguments:
- updates: float32 [256, 128, 3584], P('client', None, 'param'), as said below
- sample_counts: int32 [256], P('client'), may hold values from 16 to 1023
Outputs:
- median: float32 [128, 3584], P('client', 'param')
- shares: float32 [256], P('client')
The draws below stay inside these ranges and needn't reach their ends.
Inputs may be any that keep to these rules, and one draw needn't show every extreme that they name: `updates`: each client's update is real-valued with every entry nonzero in general.
All inputs are finite; a program needn't handle non-finite values.
Results may differ from the reference program's by a relative error of at most 0.0001.
Values sent between devices are 32-bit elements; how exact they have to be, the bound alone decides.
No kernel may reach another device: no remote copies, remote signals or barrier semaphores. Data moves between devices by JAX's collectives and lax.ppermute only.
A program may use at most 64 MiB of HBM per device.

```python
import math
import jax
import jax.numpy as jnp
from jax import lax

COLS = 3584
ROWS = 128
ITERS = 2
CLIENTS = 256


def draw_updates(key, part):
    subkeys = jax.random.split(jax.random.fold_in(key, 7), 8)
    common = jax.random.normal(subkeys[0], (ROWS, COLS), jnp.float32)
    column_scale = jnp.exp(jax.random.uniform(subkeys[1], (COLS,), jnp.float32, 0.0, math.log(10.0))) / 3.0
    client_scale = jnp.exp(jax.random.uniform(subkeys[2], (CLIENTS, ROWS, 1), jnp.float32, math.log(0.3), math.log(3.0)))
    ranking = jax.random.permutation(subkeys[4], CLIENTS)
    outlier = (ranking < CLIENTS // 5).astype(jnp.float32)
    magnitude = 3.0 * jnp.exp(jax.random.uniform(subkeys[5], (CLIENTS,), jnp.float32, 0.0, math.log(3.0)))
    direction = jax.random.normal(subkeys[6], (ROWS, COLS), jnp.float32)
    block_start = jax.random.randint(subkeys[7], (CLIENTS,), 0, ROWS).astype(jnp.int32)
    row_index = jnp.arange(ROWS, dtype=jnp.int32)
    offset = (row_index[None, :] - block_start[:, None] + ROWS) % ROWS
    in_block = (offset < max(ROWS // 8, 1)).astype(jnp.float32)
    shifted = ((outlier * magnitude)[:, None] * in_block)[:, :, None] * direction[None]
    client_noise = jax.random.normal(subkeys[3], (CLIENTS, ROWS, COLS), jnp.float32)
    return ((common + client_scale * client_noise + shifted) * column_scale).astype(jnp.float32)


def set_ends(values, stream_key, low, top_value):
    spot = [jax.random.randint(jax.random.fold_in(stream_key, axis), (), 0, length) for axis, length in enumerate(values.shape)]
    longest = values.shape.index(max(values.shape))
    neighbour = spot[:longest] + [(spot[longest] + 1) % values.shape[longest]] + spot[longest + 1:]
    return values.at[tuple(spot)].set(low).at[tuple(neighbour)].set(top_value)


def setup_inputs(seed: int = 0) -> dict:
    streams_of = jax.random.split(jax.random.key(seed), 3)
    return {
        "updates": draw_updates(jax.random.fold_in(streams_of[2], 71), 0),
        "sample_counts": set_ends(jax.random.randint(streams_of[1], (CLIENTS,), 16, 1024), jax.random.fold_in(streams_of[1], 1), 16, 1023).astype(jnp.int32),
    }


smoothing = 1e-06

def weighted_sum(weights, updates):
    return jnp.einsum('c,crk->rk', weights, updates, precision=lax.Precision.HIGHEST)

def reference(updates, sample_counts):
    counts_f = sample_counts.astype(jnp.float32)
    median = weighted_sum(counts_f, updates) / jnp.sum(counts_f)
    weights = counts_f
    weight_sum = jnp.sum(counts_f)
    for iteration in range(ITERS):
        distance_sq = lax.map(lambda client: jnp.sum((client - median) ** 2), updates)
        weights = counts_f / jnp.sqrt(distance_sq + smoothing)
        weight_sum = jnp.sum(weights)
        median = weighted_sum(weights, updates) / weight_sum
    shares = CLIENTS * weights / weight_sum
    return (median, shares)
```

```python
import jax
import jax.numpy as jnp
from jax import lax
from jax.sharding import Mesh
from jax.sharding import PartitionSpec as P

ITERS = 2
SMOOTHING = 1e-06

CLIENT = ("y", "far", "pair", "x")
PLANE = ("y", "pair", "x")
PLANE_CORES = ("y", "pair", "x", "param")
LINE = ("far", "pair")

SUBLANES = 8
LANES = 128


def spread(value, axes):
    copies = jnp.broadcast_to(value[None], (lax.axis_size(axes), *value.shape))
    return lax.all_to_all(copies, axes, 0, 0, tiled=True)


def local(updates, sample_counts):
    clients, rows, columns = updates.shape
    ny, nfar, npair, nx = (lax.axis_size(a) for a in CLIENT)
    nz = nfar * npair
    plane = ny * npair * nx
    total_clients = clients * plane * nfar
    tiles = columns // npair // LANES

    blocks = updates.reshape(clients, ny, nz, nx, npair, tiles, LANES)
    blocks = blocks.transpose(1, 4, 3, 0, 5, 2, 6).reshape(plane, clients * tiles, nz, LANES)
    counts = sample_counts.astype(jnp.float32)
    counts = jnp.broadcast_to(jnp.repeat(counts, nz // clients)[None, None, :, None], (plane, 1, nz, LANES))
    held = lax.all_to_all(jnp.concatenate([blocks, counts], axis=1), PLANE, 0, 0, tiled=True)
    counts_f = held[:, clients * tiles, :: nz // clients, 0]
    held = held[:, : clients * tiles].reshape(plane, clients, tiles, nz, LANES)

    weights = counts_f
    for iteration in range(ITERS + 1):
        partial = jnp.sum(held * weights[:, :, None, None, None], axis=(0, 1))
        weight_sum = jnp.sum(weights)
        if iteration == ITERS:
            break
        sums = jnp.concatenate([partial, jnp.broadcast_to(weight_sum, (1, nz, LANES))])
        sums = jnp.sum(spread(sums, "far"), axis=0)
        median = sums[:tiles] / sums[tiles:]
        distance_sq = jnp.sum((held - median) ** 2, axis=(2, 3, 4)).reshape(-1)
        distance_sq = jnp.pad(distance_sq, (0, LANES - distance_sq.shape[0]))
        distance_sq = jnp.sum(spread(distance_sq, PLANE_CORES), axis=0)[: plane * clients]
        weights = counts_f / jnp.sqrt(distance_sq.reshape(plane, clients) + SMOOTHING)

    last = jnp.concatenate([partial.transpose(1, 0, 2), jnp.broadcast_to(weight_sum, (nz, 1, LANES))], axis=1)
    last = lax.all_to_all(last, LINE, 0, 0, tiled=True)
    last = jnp.sum(last.reshape(nfar, npair, tiles + 1, LANES), axis=0)
    weight_sum = last[0, tiles, 0]
    median = (last[:, :tiles] / weight_sum).reshape(1, columns)
    mine = lax.dynamic_slice_in_dim(weights, lax.axis_index(PLANE), 1, 0)[0]
    return median, total_clients * mine / weight_sum


def solution(mesh):
    finer = Mesh(
        mesh.devices.reshape(4, 4, 2, 4, mesh.shape["param"]),
        ("y", "far", "pair", "x", "param"),
    )
    return jax.shard_map(
        local,
        mesh=finer,
        in_specs=(P(CLIENT, None, "param"), P(CLIENT)),
        out_specs=(P(CLIENT, "param"), P(CLIENT)),
        check_vma=False,
    )
```

```python
import functools

import jax
import jax.numpy as jnp
from jax import lax
from jax.experimental import pallas as pl
from jax.experimental.pallas import tpu as pltpu
from jax.sharding import Mesh
from jax.sharding import PartitionSpec as P

ITERS = 2
SMOOTHING = 1e-06

CLIENT = ("y", "far", "pair", "x")
PLANE = ("y", "pair", "x")
PLANE_CORES = ("y", "pair", "x", "param")
LINE = ("far", "pair")

SUB = 8
LANES = 128
VMEM = pl.BlockSpec(memory_space=pltpu.VMEM)
HBM = pl.BlockSpec(memory_space=pltpu.HBM)


def call(body, outs, in_specs, name, scratch=()):
    return pl.pallas_call(
        body,
        out_shape=outs,
        in_specs=in_specs,
        out_specs=jax.tree.map(lambda _: VMEM, outs),
        scratch_shapes=scratch,
        compiler_params=pltpu.CompilerParams(vmem_limit_bytes=8 << 20),
        name=name,
    )


def f32(*shape):
    return jax.ShapeDtypeStruct(shape, jnp.float32)


def wide(row, rows=SUB):
    return jnp.broadcast_to(row, (rows, LANES))


def pack_body(ny, nx, npair, tiles, u_hbm, counts_hbm, out, buf, counts, sems, counts_sem):
    clients, rows, _ = u_hbm.shape
    span = rows // ny

    def copy(k, j):
        n = k * npair * tiles + j
        return pltpu.make_async_copy(u_hbm.at[k, :, pl.ds(j * LANES, LANES)], buf.at[n], sems.at[n])

    fetch = pltpu.make_async_copy(counts_hbm, counts, counts_sem)
    fetch.start()
    for k in range(clients):
        for j in range(npair * tiles):
            copy(k, j).start()
    fetch.wait()
    upper = lax.broadcasted_iota(jnp.int32, (SUB, LANES), 0) >= SUB // 2
    tile = jnp.where(upper, counts[1], counts[0]).astype(jnp.float32)
    for p in range(ny * npair * nx):
        out[p, clients * tiles] = tile
    for k in range(clients):
        for j in range(npair * tiles):
            h, t = divmod(j, tiles)
            copy(k, j).wait()
            for y in range(ny):
                for x in range(nx):
                    part = buf[k * npair * tiles + j, pl.ds(y * span + x, SUB, stride=nx), :]
                    out[(y * npair + h) * nx + x, k * tiles + t] = part


def weighted(held, weights, tiles):
    plane = held.shape[0]

    def step(src, accs):
        accs = list(accs)
        for k in range(2):
            w = wide(weights[pl.ds(k * plane + src, 1), :])
            for t in range(tiles):
                accs[t] = accs[t] + w * held[src, k * tiles + t]
            accs[tiles] = accs[tiles] + w
        return tuple(accs)

    zero = jnp.zeros((SUB, LANES), jnp.float32)
    return lax.fori_loop(0, plane, step, (zero,) * (tiles + 1), unroll=8)


def take_counts(held, counts, tiles):
    plane = held.shape[0]
    for src in range(plane):
        for k in range(2):
            counts[pl.ds(k * plane + src, 1), :] = held[src, 2 * tiles, pl.ds(k * SUB // 2, 1), :]


def reweigh(held, dist, weights, tiles):
    plane = held.shape[0]
    take_counts(held, weights, tiles)
    total = jnp.sum(dist[:, 0, :], axis=0, keepdims=True)
    column = wide(total, LANES).T[: 2 * plane]
    weights[...] = weights[...] / jnp.sqrt(column + SMOOTHING)


def start_body(tiles, held, out, weights):
    take_counts(held, weights, tiles)
    sums = weighted(held, weights, tiles)
    for f in range(out.shape[0]):
        for t in range(tiles + 1):
            out[f, t] = sums[t]


def again_body(tiles, held, dist, out, weights):
    reweigh(held, dist, weights, tiles)
    sums = weighted(held, weights, tiles)
    for f in range(out.shape[0]):
        for t in range(tiles + 1):
            out[f, t] = sums[t]


def last_body(tiles, held, dist, out, mine, weights):
    plane = held.shape[0]
    reweigh(held, dist, weights, tiles)
    sums = weighted(held, weights, tiles)
    nz = out.shape[0] // SUB
    for t in range(tiles + 1):
        out[pl.ds(t, nz, stride=SUB), :] = sums[t]
    me = lax.axis_index(PLANE)
    for k in range(2):
        mine[pl.ds(k * SUB // 2, SUB // 2), :] = wide(weights[pl.ds(k * plane + me, 1), :], SUB // 2)


def distance_body(tiles, held, sums, out, rows):
    plane = held.shape[0]
    whole = [functools.reduce(jnp.add, [sums[f, t] for f in range(sums.shape[0])]) for t in range(tiles + 1)]
    median = [whole[t] / whole[tiles] for t in range(tiles)]

    def step(src, carry):
        for k in range(2):
            acc = None
            for t in range(tiles):
                diff = held[src, k * tiles + t] - median[t]
                acc = diff * diff if acc is None else acc + diff * diff
            rows[pl.ds(pl.multiple_of((k * plane + src) * SUB, SUB), SUB), :] = acc
        return carry

    lax.fori_loop(0, plane, step, 0, unroll=8)
    clients = 2 * plane
    lanes = []
    for g in range(clients // SUB):
        parts = [rows[pl.ds(g * SUB * SUB + s, SUB, stride=SUB), :] for s in range(SUB)]
        lanes.append(functools.reduce(jnp.add, parts))
    lanes = jnp.concatenate(lanes + [jnp.zeros((LANES - clients, LANES), jnp.float32)], axis=0)
    out[...] = jnp.sum(lanes.T, axis=0, keepdims=True)


def finish_body(total_clients, tiles, got, mine, median, shares):
    nfar = got.shape[0] // 2
    halves = []
    for h in range(2):
        halves.append(functools.reduce(jnp.add, [got[f * 2 + h] for f in range(nfar)]))
    total = halves[0][tiles : tiles + 1]
    for h in range(2):
        part = halves[h] / total
        for t in range(tiles):
            median[:, pl.ds((h * tiles + t) * LANES, LANES)] = part[t : t + 1]
    share = total_clients * mine[...] / total
    lane = lax.broadcasted_iota(jnp.int32, (1, LANES), 1)
    share = jnp.where(lane == 0, share[:1], share[SUB // 2 : SUB // 2 + 1])
    shares[...] = share[0, : shares.shape[0]]


def local(updates, sample_counts):
    clients, rows, columns = updates.shape
    ny, nfar, npair, nx = (lax.axis_size(a) for a in CLIENT)
    nz = nfar * npair
    plane = ny * npair * nx
    tiles = columns // npair // LANES
    bind = functools.partial

    held = call(
        bind(pack_body, ny, nx, npair, tiles),
        f32(plane, clients * tiles + 1, nz, LANES),
        [HBM, HBM],
        "pack",
        scratch=[
            pltpu.VMEM((clients * npair * tiles, rows, LANES), jnp.float32),
            pltpu.SMEM((clients,), jnp.int32),
            pltpu.SemaphoreType.DMA((clients * npair * tiles,)),
            pltpu.SemaphoreType.DMA,
        ],
    )(*(pltpu.with_memory_space_constraint(a, pltpu.HBM) for a in (updates, sample_counts)))
    held = lax.all_to_all(held, PLANE, 0, 0, tiled=True)

    rows_of_weights = [pltpu.VMEM((clients * plane, LANES), jnp.float32)]
    payload = f32(nfar, tiles + 1, nz, LANES)
    sums = call(bind(start_body, tiles), payload, [VMEM], "start", scratch=rows_of_weights)(held)
    for iteration in range(ITERS):
        sums = lax.all_to_all(sums, "far", 0, 0, tiled=True)
        dist = call(
            bind(distance_body, tiles),
            f32(1, LANES),
            [VMEM, VMEM],
            "distance",
            scratch=[pltpu.VMEM((clients * plane * SUB, LANES), jnp.float32)],
        )(held, sums)
        dist = jnp.broadcast_to(dist[None], (plane * lax.axis_size("param"), 1, LANES))
        dist = lax.all_to_all(dist, PLANE_CORES, 0, 0, tiled=True)
        if iteration < ITERS - 1:
            sums = call(bind(again_body, tiles), payload, [VMEM, VMEM], "again", scratch=rows_of_weights)(held, dist)
    last, mine = call(
        bind(last_body, tiles),
        (f32(nz * SUB, LANES), f32(SUB, LANES)),
        [VMEM, VMEM],
        "last",
        scratch=rows_of_weights,
    )(held, dist)
    last = lax.all_to_all(last.reshape(nz, SUB, LANES), LINE, 0, 0, tiled=True)
    median, shares = call(
        bind(finish_body, clients * plane * nfar, tiles),
        (f32(1, columns), f32(clients)),
        [VMEM, VMEM],
        "finish",
    )(last, mine)
    return median, shares


def solution(mesh):
    finer = Mesh(
        mesh.devices.reshape(4, 4, 2, 4, mesh.shape["param"]),
        ("y", "far", "pair", "x", "param"),
    )
    return jax.shard_map(
        local,
        mesh=finer,
        in_specs=(P(CLIENT, None, "param"), P(CLIENT)),
        out_specs=(P(CLIENT, "param"), P(CLIENT)),
        check_vma=False,
    )
```

```python
import functools

import jax
import jax.numpy as jnp
from jax import lax
from jax.experimental import pallas as pl
from jax.experimental.pallas import tpu as pltpu
from jax.sharding import Mesh
from jax.sharding import PartitionSpec as P

ITERS = 2
SMOOTHING = 1e-06

CLIENT = ("y", "far", "pair", "x")
PLANE = ("y", "pair", "x")
PLANE_CORES = ("y", "pair", "x", "param")
LINE = ("far", "pair")
GROUPS = ((0, 2, 5, 7), (1, 3, 4, 6))

SUB = 8
HALF = SUB // 2
LANES = 128
VMEM = pl.BlockSpec(memory_space=pltpu.VMEM)
HBM = pl.BlockSpec(memory_space=pltpu.HBM)


def call(body, outs, in_specs, name, scratch=()):
    return pl.pallas_call(
        body,
        out_shape=outs,
        in_specs=in_specs,
        out_specs=jax.tree.map(lambda _: VMEM, outs),
        scratch_shapes=scratch,
        compiler_params=pltpu.CompilerParams(vmem_limit_bytes=8 << 20),
        name=name,
    )


def f32(*shape):
    return jax.ShapeDtypeStruct(shape, jnp.float32)


def sublane():
    return lax.broadcasted_iota(jnp.int32, (SUB, LANES), 0)


def pack_body(tiles, u_hbm, counts_hbm, out, buf, counts, sems, counts_sem):
    clients, ny, span, _ = u_hbm.shape
    nx = span // SUB

    def copy(k, j):
        src = u_hbm.at[k, :, :, pl.ds(j * LANES, LANES)]
        return pltpu.make_async_copy(src, buf.at[j, :, pl.ds(k * span, span), :], sems.at[k, j])

    fetch = pltpu.make_async_copy(counts_hbm, counts, counts_sem)
    fetch.start()
    for j in range(tiles):
        for k in range(clients):
            copy(k, j).start()
    row = sublane()
    flip = (lax.axis_index("far") >= 2).astype(jnp.int32)
    mask = ((row >> 1) & 1) == flip
    fetch.wait()
    tile = jnp.where(row < HALF, counts[0], counts[1]).astype(jnp.float32)
    for p in range(ny * 2 * nx):
        out[p, tiles] = tile
    for j in range(tiles):
        for k in range(clients):
            copy(k, j).wait()
        for y in range(ny):
            for x in range(nx):
                even = buf[j, y, pl.ds(x, SUB, stride=2 * nx), :]
                odd = buf[j, y, pl.ds(nx + x, SUB, stride=2 * nx), :]
                out[(y * 2) * nx + x, j] = jnp.where(mask, even, odd)
                out[(y * 2 + 1) * nx + x, j] = jnp.where(mask, odd, even)


def weighted(held, weigh):
    plane, tiles = held.shape[0], held.shape[1] - 1

    def step(src, accs):
        w = weigh(src)
        sums = [accs[t] + w * held[src, t] for t in range(tiles)]
        return (*sums, accs[tiles] + w)

    zero = jnp.zeros((SUB, LANES), jnp.float32)
    accs = lax.fori_loop(0, plane, step, (zero,) * (tiles + 1), unroll=8)
    return [a + pltpu.roll(a, HALF, 0) for a in accs]


def weigh_by_count(held):
    return lambda src: held[src, held.shape[1] - 1]


def weigh_by_distance(held, dist, spread):
    clients = 2 * held.shape[0]
    total = jnp.sum(dist[:, 0, :], axis=0, keepdims=True)
    column = jnp.broadcast_to(total, (LANES, LANES)).T[:clients]
    for i in range(HALF):
        spread[pl.ds(i, clients, stride=HALF), :] = column
    counts = weigh_by_count(held)

    def weigh(src):
        at = pl.ds(pl.multiple_of(src * SUB, SUB), SUB)
        return counts(src) / jnp.sqrt(spread[at, :] + SMOOTHING)

    return weigh


def give_sums(sums, out):
    top = sublane() < HALF
    tiles = len(sums) - 1
    for g in range(out.shape[0]):
        for t in range(tiles // 2):
            out[g, t] = jnp.where(top, sums[2 * t], sums[2 * t + 1])
        out[g, tiles // 2] = sums[tiles]


def start_body(held, out):
    give_sums(weighted(held, weigh_by_count(held)), out)


def again_body(held, dist, out, spread):
    give_sums(weighted(held, weigh_by_distance(held, dist, spread)), out)


def last_body(held, dist, out, mine, spread):
    weigh = weigh_by_distance(held, dist, spread)
    sums = weighted(held, weigh)
    deep = out.shape[0] // HALF
    for t in range(deep):
        out[pl.ds(t, HALF, stride=deep), :] = sums[min(t, len(sums) - 1)][:HALF]
    mine[...] = weigh(lax.axis_index(PLANE))


def distance_body(held, sums, out, rows):
    plane, tiles = held.shape[0], held.shape[1] - 1
    whole = [functools.reduce(jnp.add, [sums[g, t] for g in range(sums.shape[0])]) for t in range(tiles // 2 + 1)]
    top = sublane() < HALF
    median = []
    for t in range(tiles // 2):
        m = whole[t] / whole[tiles // 2]
        r = pltpu.roll(m, HALF, 0)
        median += [jnp.where(top, m, r), jnp.where(top, r, m)]

    def step(src, carry):
        acc = None
        for t in range(tiles):
            diff = held[src, t] - median[t]
            acc = diff * diff if acc is None else acc + diff * diff
        rows[pl.ds(pl.multiple_of(src * SUB, SUB), SUB), :] = acc
        return carry

    lax.fori_loop(0, plane, step, 0, unroll=8)
    clients = 2 * plane
    lanes = []
    for g in range(clients // SUB):
        parts = [rows[pl.ds(g * SUB * HALF + i, SUB, stride=HALF), :] for i in range(HALF)]
        lanes.append(functools.reduce(jnp.add, parts))
    lanes = jnp.concatenate(lanes + [jnp.zeros((LANES - clients, LANES), jnp.float32)], axis=0)
    out[...] = jnp.sum(lanes.T, axis=0, keepdims=True)


def finish_body(total_clients, got, mine, median, shares):
    tiles = median.shape[1] // LANES
    whole = functools.reduce(jnp.add, [got[g] for g in range(got.shape[0])])
    total = whole[tiles : tiles + 1]
    part = whole / total
    for t in range(tiles):
        median[:, pl.ds(t * LANES, LANES)] = part[t : t + 1]
    share = total_clients * mine[...] / total
    lane = lax.broadcasted_iota(jnp.int32, (1, LANES), 1)
    share = jnp.where(lane == 0, share[:1], share[HALF : HALF + 1])
    shares[...] = share[0, : shares.shape[0]]


def local(updates, sample_counts):
    clients, rows, columns = updates.shape
    ny, nfar, npair, nx = (lax.axis_size(a) for a in CLIENT)
    plane = ny * npair * nx
    tiles = columns // LANES
    deep = 2 * SUB

    updates = updates.reshape(clients, ny, rows // ny, columns)
    held = call(
        functools.partial(pack_body, tiles),
        f32(plane, tiles + 1, SUB, LANES),
        [HBM, HBM],
        "pack",
        scratch=[
            pltpu.VMEM((tiles, ny, clients * (rows // ny), LANES), jnp.float32),
            pltpu.SMEM((clients,), jnp.int32),
            pltpu.SemaphoreType.DMA((clients, tiles)),
            pltpu.SemaphoreType.DMA,
        ],
    )(*(pltpu.with_memory_space_constraint(a, pltpu.HBM) for a in (updates, sample_counts)))
    held = lax.all_to_all(held, PLANE, 0, 0, tiled=True)

    per_row = [pltpu.VMEM((plane * SUB, LANES), jnp.float32)]
    payload = f32(nfar, tiles // 2 + 1, SUB, LANES)
    along_z = functools.partial(
        lax.all_to_all, axis_name=LINE, split_axis=0, concat_axis=0, tiled=True, axis_index_groups=GROUPS
    )
    sums = call(start_body, payload, [VMEM], "start")(held)
    for iteration in range(ITERS):
        dist = call(distance_body, f32(1, LANES), [VMEM, VMEM], "distance", scratch=per_row)(held, along_z(sums))
        dist = jnp.broadcast_to(dist[None], (plane * lax.axis_size("param"), 1, LANES))
        dist = lax.all_to_all(dist, PLANE_CORES, 0, 0, tiled=True)
        if iteration < ITERS - 1:
            sums = call(again_body, payload, [VMEM, VMEM], "again", scratch=per_row)(held, dist)
    last, mine = call(
        last_body, (f32(nfar * deep, LANES), f32(SUB, LANES)), [VMEM, VMEM], "last", scratch=per_row
    )(held, dist)
    median, shares = call(
        functools.partial(finish_body, clients * plane * nfar), (f32(1, columns), f32(clients)), [VMEM, VMEM], "finish"
    )(along_z(last.reshape(nfar, deep, LANES)), mine)
    return median, shares


def solution(mesh):
    finer = Mesh(
        mesh.devices.reshape(4, 4, 2, 4, mesh.shape["param"]),
        ("y", "far", "pair", "x", "param"),
    )
    return jax.shard_map(
        local,
        mesh=finer,
        in_specs=(P(CLIENT, None, "param"), P(CLIENT)),
        out_specs=(P(CLIENT, "param"), P(CLIENT)),
        check_vma=False,
    )
```

```python
import functools

import jax
import jax.numpy as jnp
from jax import lax
from jax.experimental import pallas as pl
from jax.experimental.pallas import tpu as pltpu
from jax.sharding import Mesh
from jax.sharding import PartitionSpec as P

ITERS = 2
SMOOTHING = 1e-06

CLIENT = ("y", "far", "pair", "x")
PLANE = ("y", "pair", "x")
PLANE_CORES = ("y", "pair", "x", "param")
LINE = ("far", "pair")
GROUPS = ((0, 2, 5, 7), (1, 3, 4, 6))

SUB = 8
HALF = SUB // 2
LANES = 128
VMEM = pl.BlockSpec(memory_space=pltpu.VMEM)
HBM = pl.BlockSpec(memory_space=pltpu.HBM)


def call(body, outs, in_specs, name, scratch=(), out_specs=None):
    return pl.pallas_call(
        body,
        out_shape=outs,
        in_specs=in_specs,
        out_specs=jax.tree.map(lambda _: VMEM, outs) if out_specs is None else out_specs,
        scratch_shapes=scratch,
        compiler_params=pltpu.CompilerParams(vmem_limit_bytes=8 << 20),
        name=name,
    )


def f32(*shape):
    return jax.ShapeDtypeStruct(shape, jnp.float32)


def sublane():
    return lax.broadcasted_iota(jnp.int32, (SUB, LANES), 0)


def pack_body(tiles, u_hbm, out_hbm, buf, out, sems, out_sems):
    clients, ny, span, _ = u_hbm.shape
    nx = span // SUB

    def copy(k, j):
        src = u_hbm.at[k, :, :, pl.ds(j * LANES, LANES)]
        return pltpu.make_async_copy(src, buf.at[j, :, pl.ds(k * span, span), :], sems.at[k, j])

    def send(j):
        return pltpu.make_async_copy(out.at[j], out_hbm.at[:, j], out_sems.at[j])

    for j in range(tiles):
        for k in range(clients):
            copy(k, j).start()
    flip = (lax.axis_index("far") >= 2).astype(jnp.int32)
    mask = ((sublane() >> 1) & 1) == flip
    for j in range(tiles):
        for k in range(clients):
            copy(k, j).wait()
        for y in range(ny):
            for x in range(nx):
                even = buf[j, y, pl.ds(x, SUB, stride=2 * nx), :]
                odd = buf[j, y, pl.ds(nx + x, SUB, stride=2 * nx), :]
                out[j, (y * 2) * nx + x] = jnp.where(mask, even, odd)
                out[j, (y * 2 + 1) * nx + x] = jnp.where(mask, odd, even)
        if j:
            send(j - 1).start()
    send(tiles - 1).start()
    for j in range(tiles):
        send(j).wait()


def weighted(held, weigh):
    plane, tiles = held.shape[0], held.shape[1]

    def step(src, accs):
        w = weigh(src)
        sums = [accs[t] + w * held[src, t] for t in range(tiles)]
        return (*sums, accs[tiles] + w)

    zero = jnp.zeros((SUB, LANES), jnp.float32)
    accs = lax.fori_loop(0, plane, step, (zero,) * (tiles + 1), unroll=8)
    return [a + pltpu.roll(a, HALF, 0) for a in accs]


def per_client(row, spread):
    clients = spread.shape[0] // HALF
    column = jnp.broadcast_to(row, (LANES, LANES)).T[:clients]
    for i in range(HALF):
        spread[pl.ds(i, clients, stride=HALF), :] = column
    return lambda src: spread[pl.ds(pl.multiple_of(src * SUB, SUB), SUB), :]


def weigh_by_distance(counts, dist, spread):
    lane = lax.broadcasted_iota(jnp.int32, (1, LANES), 1)
    total = jnp.sum(dist[:, 0, :], axis=0, keepdims=True)
    weight = counts[...] / jnp.sqrt(jnp.where(lane < spread.shape[0] // HALF, total, 1.0) + SMOOTHING)
    return per_client(weight, spread)


def give_sums(sums, out):
    top = sublane() < HALF
    tiles = len(sums) - 1
    for g in range(out.shape[0]):
        for t in range(tiles // 2):
            out[g, t] = jnp.where(top, sums[2 * t], sums[2 * t + 1])
        out[g, tiles // 2] = sums[tiles]


def start_body(held, counts, out, spread):
    give_sums(weighted(held, per_client(counts[...], spread)), out)


def again_body(held, counts, dist, out, spread):
    give_sums(weighted(held, weigh_by_distance(counts, dist, spread)), out)


def last_body(held, counts, dist, out, mine, spread):
    weigh = weigh_by_distance(counts, dist, spread)
    sums = weighted(held, weigh)
    deep = out.shape[0] // HALF
    for t in range(deep):
        out[pl.ds(t, HALF, stride=deep), :] = sums[min(t, len(sums) - 1)][:HALF]
    mine[...] = weigh(lax.axis_index(PLANE))


def distance_body(held, sums, out, rows):
    plane, tiles = held.shape[0], held.shape[1]
    whole = [functools.reduce(jnp.add, [sums[g, t] for g in range(sums.shape[0])]) for t in range(tiles // 2 + 1)]
    top = sublane() < HALF
    median = []
    for t in range(tiles // 2):
        m = whole[t] / whole[tiles // 2]
        r = pltpu.roll(m, HALF, 0)
        median += [jnp.where(top, m, r), jnp.where(top, r, m)]

    def step(src, carry):
        acc = None
        for t in range(tiles):
            diff = held[src, t] - median[t]
            acc = diff * diff if acc is None else acc + diff * diff
        rows[pl.ds(pl.multiple_of(src * SUB, SUB), SUB), :] = acc
        return carry

    lax.fori_loop(0, plane, step, 0, unroll=8)
    clients = 2 * plane
    lanes = []
    for g in range(clients // SUB):
        parts = [rows[pl.ds(g * SUB * HALF + i, SUB, stride=HALF), :] for i in range(HALF)]
        lanes.append(functools.reduce(jnp.add, parts))
    lanes = jnp.concatenate(lanes + [jnp.zeros((LANES - clients, LANES), jnp.float32)], axis=0)
    out[...] = jnp.sum(lanes.T, axis=0, keepdims=True)


def finish_body(total_clients, got, mine, median, shares):
    tiles = median.shape[1] // LANES
    whole = functools.reduce(jnp.add, [got[g] for g in range(got.shape[0])])
    total = whole[tiles : tiles + 1]
    part = whole / total
    for t in range(tiles):
        median[:, pl.ds(t * LANES, LANES)] = part[t : t + 1]
    share = total_clients * mine[...] / total
    lane = lax.broadcasted_iota(jnp.int32, (1, LANES), 1)
    share = jnp.where(lane == 0, share[:1], share[HALF : HALF + 1])
    shares[...] = share[0, : shares.shape[0]]


def local(updates, sample_counts):
    clients, rows, columns = updates.shape
    ny, nfar, npair, nx = (lax.axis_size(a) for a in CLIENT)
    plane = ny * npair * nx
    tiles = columns // LANES
    deep = 2 * SUB

    updates = updates.reshape(clients, ny, rows // ny, columns)
    held = call(
        functools.partial(pack_body, tiles),
        pltpu.HBM((plane, tiles, SUB, LANES), jnp.float32),
        [HBM],
        "pack",
        out_specs=HBM,
        scratch=[
            pltpu.VMEM((tiles, ny, clients * (rows // ny), LANES), jnp.float32),
            pltpu.VMEM((tiles, plane, SUB, LANES), jnp.float32),
            pltpu.SemaphoreType.DMA((clients, tiles)),
            pltpu.SemaphoreType.DMA((tiles,)),
        ],
    )(pltpu.with_memory_space_constraint(updates, pltpu.HBM))
    held = lax.all_to_all(held, PLANE, 0, 0, tiled=True)

    lane = jnp.arange(LANES) - lax.axis_index(PLANE) * clients
    counts = sample_counts.astype(jnp.float32)
    counts = jnp.where(lane == 0, counts[0], jnp.where(lane == 1, counts[1], 0.0))[None]
    counts = counts + lax.ppermute(counts, "pair", ((0, 1), (1, 0)))
    for axis in ("y", "x"):
        counts = lax.psum(counts, axis)

    per_row = [pltpu.VMEM((plane * SUB, LANES), jnp.float32)]
    payload = f32(nfar, tiles // 2 + 1, SUB, LANES)
    along_z = functools.partial(
        lax.all_to_all, axis_name=LINE, split_axis=0, concat_axis=0, tiled=True, axis_index_groups=GROUPS
    )
    sums = call(start_body, payload, [VMEM, VMEM], "start", scratch=per_row)(held, counts)
    for iteration in range(ITERS):
        dist = call(distance_body, f32(1, LANES), [VMEM, VMEM], "distance", scratch=per_row)(held, along_z(sums))
        dist = jnp.broadcast_to(dist[None], (plane * lax.axis_size("param"), 1, LANES))
        dist = lax.all_to_all(dist, PLANE_CORES, 0, 0, tiled=True)
        if iteration < ITERS - 1:
            sums = call(again_body, payload, [VMEM] * 3, "again", scratch=per_row)(held, counts, dist)
    last, mine = call(
        last_body, (f32(nfar * deep, LANES), f32(SUB, LANES)), [VMEM] * 3, "last", scratch=per_row
    )(held, counts, dist)
    median, shares = call(
        functools.partial(finish_body, clients * plane * nfar), (f32(1, columns), f32(clients)), [VMEM, VMEM], "finish"
    )(along_z(last.reshape(nfar, deep, LANES)), mine)
    return median, shares


def solution(mesh):
    finer = Mesh(
        mesh.devices.reshape(4, 4, 2, 4, mesh.shape["param"]),
        ("y", "far", "pair", "x", "param"),
    )
    return jax.shard_map(
        local,
        mesh=finer,
        in_specs=(P(CLIENT, None, "param"), P(CLIENT)),
        out_specs=(P(CLIENT, "param"), P(CLIENT)),
        check_vma=False,
    )
```

```python
import functools

import jax
import jax.numpy as jnp
from jax import lax
from jax.experimental import pallas as pl
from jax.experimental.pallas import tpu as pltpu
from jax.sharding import Mesh
from jax.sharding import PartitionSpec as P

ITERS = 2
SMOOTHING = 1e-06

CLIENT = ("y", "far", "pair", "x")
PLANE = ("y", "pair", "x")
PLANE_CORES = ("y", "pair", "x", "param")
LINE = ("far", "pair")
GROUPS = ((0, 2, 5, 7), (1, 3, 4, 6))


def place(y, pair, x):
    return (pair + x) % 2 * 16 + (y + 4 - x) % 4 * 4 + x


def planes():
    order = sorted((place(y, p, x), y, p, x) for y in range(4) for p in range(2) for x in range(4))
    return tuple(tuple(((y * 4 + f) * 2 + p) * 4 + x for _, y, p, x in order) for f in range(4))


SUB = 8
HALF = SUB // 2
LANES = 128
VMEM = pl.BlockSpec(memory_space=pltpu.VMEM)
HBM = pl.BlockSpec(memory_space=pltpu.HBM)


def call(body, outs, in_specs, name, scratch=()):
    return pl.pallas_call(
        body,
        out_shape=outs,
        in_specs=in_specs,
        out_specs=jax.tree.map(lambda _: VMEM, outs),
        scratch_shapes=scratch,
        compiler_params=pltpu.CompilerParams(vmem_limit_bytes=8 << 20),
        name=name,
    )


def f32(*shape):
    return jax.ShapeDtypeStruct(shape, jnp.float32)


def sublane():
    return lax.broadcasted_iota(jnp.int32, (SUB, LANES), 0)


def pack_body(tiles, u_hbm, counts_hbm, out, buf, counts, sems, counts_sem):
    clients, ny, span, _ = u_hbm.shape
    step = tiles * SUB
    nx = HALF

    def copy(k, y):
        return pltpu.make_async_copy(u_hbm.at[k, y], buf.at[y, pl.ds(k * span, span), :], sems.at[k, y])

    fetch = pltpu.make_async_copy(counts_hbm, counts, counts_sem)
    fetch.start()
    for y in range(ny):
        for k in range(clients):
            copy(k, y).start()
    row = sublane()
    flip = (lax.axis_index("far") >= 2).astype(jnp.int32)
    mask = ((row >> 1) & 1) == flip
    fetch.wait()
    tile = jnp.where(row < HALF, counts[0], counts[1]).astype(jnp.float32)
    for p in range(out.shape[0]):
        out[p, tiles] = tile
    for y in range(ny):
        for k in range(clients):
            copy(k, y).wait()
        for x in range(nx):
            for t in range(tiles):
                even = buf[y, pl.ds(t * SUB + x, SUB, stride=step), :]
                odd = buf[y, pl.ds(t * SUB + nx + x, SUB, stride=step), :]
                out[place(y, 0, x), t] = jnp.where(mask, even, odd)
                out[place(y, 1, x), t] = jnp.where(mask, odd, even)


def weighted(held, weigh):
    plane, tiles = held.shape[0], held.shape[1] - 1

    def step(src, accs):
        w = weigh(src)
        sums = [accs[t] + w * held[src, t] for t in range(tiles)]
        return (*sums, accs[tiles] + w)

    zero = jnp.zeros((SUB, LANES), jnp.float32)
    accs = lax.fori_loop(0, plane, step, (zero,) * (tiles + 1), unroll=8)
    return [a + pltpu.roll(a, HALF, 0) for a in accs]


def weigh_by_count(held):
    return lambda src: held[src, held.shape[1] - 1]


def weigh_by_distance(held, dist, spread):
    clients = 2 * held.shape[0]
    total = jnp.sum(dist[:, 0, :], axis=0, keepdims=True)
    column = jnp.broadcast_to(total, (LANES, LANES)).T[:clients]
    for i in range(HALF):
        spread[pl.ds(i, clients, stride=HALF), :] = column
    counts = weigh_by_count(held)

    def weigh(src):
        at = pl.ds(pl.multiple_of(src * SUB, SUB), SUB)
        return counts(src) / jnp.sqrt(spread[at, :] + SMOOTHING)

    return weigh


def give_sums(sums, out):
    top = sublane() < HALF
    tiles = len(sums) - 1
    for g in range(out.shape[0]):
        for t in range(tiles // 2):
            out[g, t] = jnp.where(top, sums[2 * t], sums[2 * t + 1])
        out[g, tiles // 2] = sums[tiles]


def start_body(held, out):
    give_sums(weighted(held, weigh_by_count(held)), out)


def again_body(held, dist, out, spread):
    give_sums(weighted(held, weigh_by_distance(held, dist, spread)), out)


def last_body(held, dist, out, mine, spread):
    weigh = weigh_by_distance(held, dist, spread)
    sums = weighted(held, weigh)
    deep = out.shape[0] // HALF
    for t in range(deep):
        out[pl.ds(t, HALF, stride=deep), :] = sums[min(t, len(sums) - 1)][:HALF]
    mine[...] = weigh(place(*(lax.axis_index(a) for a in PLANE)))


def distance_body(held, sums, out, rows):
    plane, tiles = held.shape[0], held.shape[1] - 1
    whole = [functools.reduce(jnp.add, [sums[g, t] for g in range(sums.shape[0])]) for t in range(tiles // 2 + 1)]
    top = sublane() < HALF
    median = []
    for t in range(tiles // 2):
        m = whole[t] / whole[tiles // 2]
        r = pltpu.roll(m, HALF, 0)
        median += [jnp.where(top, m, r), jnp.where(top, r, m)]

    def step(src, carry):
        acc = None
        for t in range(tiles):
            diff = held[src, t] - median[t]
            acc = diff * diff if acc is None else acc + diff * diff
        rows[pl.ds(pl.multiple_of(src * SUB, SUB), SUB), :] = acc
        return carry

    lax.fori_loop(0, plane, step, 0, unroll=8)
    clients = 2 * plane
    lanes = []
    for g in range(clients // SUB):
        parts = [rows[pl.ds(g * SUB * HALF + i, SUB, stride=HALF), :] for i in range(HALF)]
        lanes.append(functools.reduce(jnp.add, parts))
    lanes = jnp.concatenate(lanes + [jnp.zeros((LANES - clients, LANES), jnp.float32)], axis=0)
    out[...] = jnp.sum(lanes.T, axis=0, keepdims=True)


def finish_body(total_clients, got, mine, median, shares):
    tiles = median.shape[1] // LANES
    whole = functools.reduce(jnp.add, [got[g] for g in range(got.shape[0])])
    total = whole[tiles : tiles + 1]
    part = whole / total
    for t in range(tiles):
        median[:, pl.ds(t * LANES, LANES)] = part[t : t + 1]
    share = total_clients * mine[...] / total
    lane = lax.broadcasted_iota(jnp.int32, (1, LANES), 1)
    share = jnp.where(lane == 0, share[:1], share[HALF : HALF + 1])
    shares[...] = share[0, : shares.shape[0]]


def local(updates, sample_counts):
    clients, rows, columns = updates.shape
    ny, nfar, npair, nx = (lax.axis_size(a) for a in CLIENT)
    plane = ny * npair * nx
    tiles = columns // LANES
    deep = 2 * SUB

    updates = updates.reshape(clients, rows // SUB, SUB, tiles, LANES).transpose(0, 1, 3, 2, 4)
    updates = updates.reshape(clients, ny, rows // ny * tiles, LANES)
    held = call(
        functools.partial(pack_body, tiles),
        f32(plane, tiles + 1, SUB, LANES),
        [HBM, HBM],
        "pack",
        scratch=[
            pltpu.VMEM((ny, clients * (rows // ny) * tiles, LANES), jnp.float32),
            pltpu.SMEM((clients,), jnp.int32),
            pltpu.SemaphoreType.DMA((clients, ny)),
            pltpu.SemaphoreType.DMA,
        ],
    )(*(pltpu.with_memory_space_constraint(a, pltpu.HBM) for a in (updates, sample_counts)))
    held = lax.all_to_all(held, CLIENT, 0, 0, tiled=True, axis_index_groups=planes())

    per_row = [pltpu.VMEM((plane * SUB, LANES), jnp.float32)]
    payload = f32(nfar, tiles // 2 + 1, SUB, LANES)
    along_z = functools.partial(
        lax.all_to_all, axis_name=LINE, split_axis=0, concat_axis=0, tiled=True, axis_index_groups=GROUPS
    )
    sums = call(start_body, payload, [VMEM], "start")(held)
    for iteration in range(ITERS):
        dist = call(distance_body, f32(1, LANES), [VMEM, VMEM], "distance", scratch=per_row)(held, along_z(sums))
        dist = jnp.broadcast_to(dist[None], (plane * lax.axis_size("param"), 1, LANES))
        dist = lax.all_to_all(dist, PLANE_CORES, 0, 0, tiled=True)
        if iteration < ITERS - 1:
            sums = call(again_body, payload, [VMEM, VMEM], "again", scratch=per_row)(held, dist)
    last, mine = call(
        last_body, (f32(nfar * deep, LANES), f32(SUB, LANES)), [VMEM, VMEM], "last", scratch=per_row
    )(held, dist)
    median, shares = call(
        functools.partial(finish_body, clients * plane * nfar), (f32(1, columns), f32(clients)), [VMEM, VMEM], "finish"
    )(along_z(last.reshape(nfar, deep, LANES)), mine)
    return median, shares


def solution(mesh):
    finer = Mesh(
        mesh.devices.reshape(4, 4, 2, 4, mesh.shape["param"]),
        ("y", "far", "pair", "x", "param"),
    )
    return jax.shard_map(
        local,
        mesh=finer,
        in_specs=(P(CLIENT, None, "param"), P(CLIENT)),
        out_specs=(P(CLIENT, "param"), P(CLIENT)),
        check_vma=False,
    )
```

```python
import functools

import jax
import jax.numpy as jnp
from jax import lax
from jax.experimental import pallas as pl
from jax.experimental.pallas import tpu as pltpu
from jax.sharding import Mesh
from jax.sharding import PartitionSpec as P

ITERS = 2
SMOOTHING = 1e-06

CLIENT = ("y", "far", "pair", "x")
PLANE = ("y", "pair", "x")
PLANE_CORES = ("y", "pair", "x", "param")
LINE = ("far", "pair")
GROUPS = ((0, 2, 5, 7), (1, 3, 4, 6))
FAR_FIRST = ((0, 5, 2, 7), (4, 1, 6, 3))


def place(y, pair, x):
    return (pair + x) % 2 * 16 + (y + 4 - x) % 4 * 4 + x


def planes():
    order = sorted((place(y, p, x), y, p, x) for y in range(4) for p in range(2) for x in range(4))
    return tuple(tuple(((y * 4 + f) * 2 + p) * 4 + x for _, y, p, x in order) for f in range(4))


SUB = 8
HALF = SUB // 2
LANES = 128
VMEM = pl.BlockSpec(memory_space=pltpu.VMEM)
HBM = pl.BlockSpec(memory_space=pltpu.HBM)


def call(body, outs, in_specs, name, scratch=()):
    return pl.pallas_call(
        body,
        out_shape=outs,
        in_specs=in_specs,
        out_specs=jax.tree.map(lambda _: VMEM, outs),
        scratch_shapes=scratch,
        compiler_params=pltpu.CompilerParams(vmem_limit_bytes=8 << 20),
        name=name,
    )


def f32(*shape):
    return jax.ShapeDtypeStruct(shape, jnp.float32)


def sublane():
    return lax.broadcasted_iota(jnp.int32, (SUB, LANES), 0)


def pack_body(tiles, u_hbm, counts_hbm, out, buf, counts, sems, counts_sem):
    clients, ny, span, _ = u_hbm.shape
    step = tiles * SUB
    nx = HALF

    def copy(k, y):
        return pltpu.make_async_copy(u_hbm.at[k, y], buf.at[y, pl.ds(k * span, span), :], sems.at[k, y])

    fetch = pltpu.make_async_copy(counts_hbm, counts, counts_sem)
    fetch.start()
    for y in range(ny):
        for k in range(clients):
            copy(k, y).start()
    row = sublane()
    flip = (lax.axis_index("far") >= 2).astype(jnp.int32)
    mask = ((row >> 1) & 1) == flip
    fetch.wait()
    tile = jnp.where(row < HALF, counts[0], counts[1]).astype(jnp.float32)
    for p in range(out.shape[0]):
        out[p, tiles] = tile
    for y in range(ny):
        for k in range(clients):
            copy(k, y).wait()
        for x in range(nx):
            for t in range(tiles):
                even = buf[y, pl.ds(t * SUB + x, SUB, stride=step), :]
                odd = buf[y, pl.ds(t * SUB + nx + x, SUB, stride=step), :]
                out[place(y, 0, x), t] = jnp.where(mask, even, odd)
                out[place(y, 1, x), t] = jnp.where(mask, odd, even)


def weighted(held, weigh):
    plane, tiles = held.shape[0], held.shape[1] - 1

    def step(src, accs):
        w = weigh(src)
        sums = [accs[t] + w * held[src, t] for t in range(tiles)]
        return (*sums, accs[tiles] + w)

    zero = jnp.zeros((SUB, LANES), jnp.float32)
    accs = lax.fori_loop(0, plane, step, (zero,) * (tiles + 1), unroll=8)
    return [a + pltpu.roll(a, HALF, 0) for a in accs]


def weigh_by_count(held):
    return lambda src: held[src, held.shape[1] - 1]


def weigh_by_distance(held, dist, spread):
    clients = 2 * held.shape[0]
    total = jnp.sum(dist[:, 0, :], axis=0, keepdims=True)
    column = jnp.broadcast_to(total, (LANES, LANES)).T[:clients]
    for i in range(HALF):
        spread[pl.ds(i, clients, stride=HALF), :] = column
    counts = weigh_by_count(held)

    def weigh(src):
        at = pl.ds(pl.multiple_of(src * SUB, SUB), SUB)
        return counts(src) / jnp.sqrt(spread[at, :] + SMOOTHING)

    return weigh


def give_sums(sums, out):
    top = sublane() < HALF
    tiles = len(sums) - 1
    for g in range(out.shape[0]):
        for t in range(tiles // 2):
            out[g, t] = jnp.where(top, sums[2 * t], sums[2 * t + 1])
        out[g, tiles // 2] = sums[tiles]


def start_body(held, out):
    give_sums(weighted(held, weigh_by_count(held)), out)


def again_body(held, dist, out, spread):
    give_sums(weighted(held, weigh_by_distance(held, dist, spread)), out)


def last_body(held, dist, out, mine, spread):
    weigh = weigh_by_distance(held, dist, spread)
    sums = weighted(held, weigh)
    deep = out.shape[0] // HALF
    for t in range(deep):
        out[pl.ds(t, HALF, stride=deep), :] = sums[min(t, len(sums) - 1)][:HALF]
    mine[...] = weigh(place(*(lax.axis_index(a) for a in PLANE)))


def distance_body(held, sums, out, rows):
    plane, tiles = held.shape[0], held.shape[1] - 1
    whole = [functools.reduce(jnp.add, [sums[g, t] for g in range(sums.shape[0])]) for t in range(tiles // 2 + 1)]
    top = sublane() < HALF
    median = []
    for t in range(tiles // 2):
        m = whole[t] / whole[tiles // 2]
        r = pltpu.roll(m, HALF, 0)
        median += [jnp.where(top, m, r), jnp.where(top, r, m)]

    def step(src, carry):
        acc = None
        for t in range(tiles):
            diff = held[src, t] - median[t]
            acc = diff * diff if acc is None else acc + diff * diff
        rows[pl.ds(pl.multiple_of(src * SUB, SUB), SUB), :] = acc
        return carry

    lax.fori_loop(0, plane, step, 0, unroll=8)
    clients = 2 * plane
    lanes = []
    for g in range(clients // SUB):
        parts = [rows[pl.ds(g * SUB * HALF + i, SUB, stride=HALF), :] for i in range(HALF)]
        lanes.append(functools.reduce(jnp.add, parts))
    lanes = jnp.concatenate(lanes + [jnp.zeros((LANES - clients, LANES), jnp.float32)], axis=0)
    out[...] = jnp.sum(lanes.T, axis=0, keepdims=True)


def finish_body(total_clients, got, mine, median, shares):
    tiles = median.shape[1] // LANES
    whole = functools.reduce(jnp.add, [got[g] for g in range(got.shape[0])])
    total = whole[tiles : tiles + 1]
    part = whole / total
    for t in range(tiles):
        median[:, pl.ds(t * LANES, LANES)] = part[t : t + 1]
    share = total_clients * mine[...] / total
    lane = lax.broadcasted_iota(jnp.int32, (1, LANES), 1)
    share = jnp.where(lane == 0, share[:1], share[HALF : HALF + 1])
    shares[...] = share[0, : shares.shape[0]]


def along_z(value, groups):
    return lax.all_to_all(value, LINE, 0, 0, tiled=True, axis_index_groups=groups)


def local(updates, sample_counts):
    clients, rows, columns = updates.shape
    ny, nfar, npair, nx = (lax.axis_size(a) for a in CLIENT)
    plane = ny * npair * nx
    tiles = columns // LANES
    deep = 2 * SUB

    updates = updates.reshape(clients, rows // SUB, SUB, tiles, LANES).transpose(0, 1, 3, 2, 4)
    updates = updates.reshape(clients, ny, rows // ny * tiles, LANES)
    held = call(
        functools.partial(pack_body, tiles),
        f32(plane, tiles + 1, SUB, LANES),
        [HBM, HBM],
        "pack",
        scratch=[
            pltpu.VMEM((ny, clients * (rows // ny) * tiles, LANES), jnp.float32),
            pltpu.SMEM((clients,), jnp.int32),
            pltpu.SemaphoreType.DMA((clients, ny)),
            pltpu.SemaphoreType.DMA,
        ],
    )(*(pltpu.with_memory_space_constraint(a, pltpu.HBM) for a in (updates, sample_counts)))
    held = lax.all_to_all(held, CLIENT, 0, 0, tiled=True, axis_index_groups=planes())

    per_row = [pltpu.VMEM((plane * SUB, LANES), jnp.float32)]
    payload = f32(nfar, tiles // 2 + 1, SUB, LANES)
    sums = call(start_body, payload, [VMEM], "start")(held)
    for iteration in range(ITERS):
        dist = call(distance_body, f32(1, LANES), [VMEM, VMEM], "distance", scratch=per_row)(held, along_z(sums, FAR_FIRST))
        dist = jnp.broadcast_to(dist[None], (plane * lax.axis_size("param"), 1, LANES))
        dist = lax.all_to_all(dist, PLANE_CORES, 0, 0, tiled=True)
        if iteration < ITERS - 1:
            sums = call(again_body, payload, [VMEM, VMEM], "again", scratch=per_row)(held, dist)
    last, mine = call(
        last_body, (f32(nfar * deep, LANES), f32(SUB, LANES)), [VMEM, VMEM], "last", scratch=per_row
    )(held, dist)
    median, shares = call(
        functools.partial(finish_body, clients * plane * nfar), (f32(1, columns), f32(clients)), [VMEM, VMEM], "finish"
    )(along_z(last.reshape(nfar, deep, LANES), GROUPS), mine)
    return median, shares


def solution(mesh):
    finer = Mesh(
        mesh.devices.reshape(4, 4, 2, 4, mesh.shape["param"]),
        ("y", "far", "pair", "x", "param"),
    )
    return jax.shard_map(
        local,
        mesh=finer,
        in_specs=(P(CLIENT, None, "param"), P(CLIENT)),
        out_specs=(P(CLIENT, "param"), P(CLIENT)),
        check_vma=False,
    )
```

```python
import functools

import jax
import jax.numpy as jnp
from jax import lax
from jax.experimental import pallas as pl
from jax.experimental.pallas import tpu as pltpu
from jax.sharding import Mesh
from jax.sharding import PartitionSpec as P

ITERS = 2
SMOOTHING = 1e-06

CLIENT = ("y", "far", "pair", "x")
PLANE = ("y", "pair", "x")
PLANE_CORES = ("y", "pair", "x", "param")
LINE = ("far", "pair")
FAR_FIRST = ((0, 5, 2, 7), (4, 1, 6, 3))


def place(y, pair, x):
    return (pair + x) % 2 * 16 + (y + 4 - x) % 4 * 4 + x


def planes():
    order = sorted((place(y, p, x), y, p, x) for y in range(4) for p in range(2) for x in range(4))
    return tuple(tuple(((y * 4 + f) * 2 + p) * 4 + x for _, y, p, x in order) for f in range(4))


SUB = 8
HALF = SUB // 2
LANES = 128
VMEM = pl.BlockSpec(memory_space=pltpu.VMEM)
HBM = pl.BlockSpec(memory_space=pltpu.HBM)


def call(body, outs, in_specs, name, scratch=()):
    return pl.pallas_call(
        body,
        out_shape=outs,
        in_specs=in_specs,
        out_specs=jax.tree.map(lambda _: VMEM, outs),
        scratch_shapes=scratch,
        compiler_params=pltpu.CompilerParams(vmem_limit_bytes=8 << 20),
        name=name,
    )


def f32(*shape):
    return jax.ShapeDtypeStruct(shape, jnp.float32)


def sublane():
    return lax.broadcasted_iota(jnp.int32, (SUB, LANES), 0)


def pack_body(tiles, u_hbm, counts_hbm, out, buf, counts, sems, counts_sem):
    clients, ny, span, _ = u_hbm.shape
    step = tiles * SUB
    nx = HALF

    def copy(k, y):
        return pltpu.make_async_copy(u_hbm.at[k, y], buf.at[y, pl.ds(k * span, span), :], sems.at[k, y])

    fetch = pltpu.make_async_copy(counts_hbm, counts, counts_sem)
    fetch.start()
    for y in range(ny):
        for k in range(clients):
            copy(k, y).start()
    row = sublane()
    flip = (lax.axis_index("far") >= 2).astype(jnp.int32)
    mask = ((row >> 1) & 1) == flip
    fetch.wait()
    tile = jnp.where(row < HALF, counts[0], counts[1]).astype(jnp.float32)
    for p in range(out.shape[0]):
        out[p, tiles] = tile
    for y in range(ny):
        for k in range(clients):
            copy(k, y).wait()
        for x in range(nx):
            for t in range(tiles):
                even = buf[y, pl.ds(t * SUB + x, SUB, stride=step), :]
                odd = buf[y, pl.ds(t * SUB + nx + x, SUB, stride=step), :]
                out[place(y, 0, x), t] = jnp.where(mask, even, odd)
                out[place(y, 1, x), t] = jnp.where(mask, odd, even)


def weighted(held, weigh):
    plane, tiles = held.shape[0], held.shape[1] - 1

    def step(src, accs):
        w = weigh(src)
        sums = [accs[t] + w * held[src, t] for t in range(tiles)]
        return (*sums, accs[tiles] + w)

    zero = jnp.zeros((SUB, LANES), jnp.float32)
    accs = lax.fori_loop(0, plane, step, (zero,) * (tiles + 1), unroll=8)
    return [a + pltpu.roll(a, HALF, 0) for a in accs]


def weigh_by_count(held):
    return lambda src: held[src, held.shape[1] - 1]


def weigh_by_distance(held, dist, spread):
    clients = 2 * held.shape[0]
    total = jnp.sum(dist[:, 0, :], axis=0, keepdims=True)
    column = jnp.broadcast_to(total, (LANES, LANES)).T[:clients]
    for i in range(HALF):
        spread[pl.ds(i, clients, stride=HALF), :] = column
    counts = weigh_by_count(held)

    def weigh(src):
        at = pl.ds(pl.multiple_of(src * SUB, SUB), SUB)
        return counts(src) / jnp.sqrt(spread[at, :] + SMOOTHING)

    return weigh


def give_sums(sums, out):
    top = sublane() < HALF
    tiles = len(sums) - 1
    for g in range(out.shape[0]):
        for t in range(tiles // 2):
            out[g, t] = jnp.where(top, sums[2 * t], sums[2 * t + 1])
        out[g, tiles // 2] = sums[tiles]


def start_body(held, out):
    give_sums(weighted(held, weigh_by_count(held)), out)


def again_body(held, dist, out, spread):
    give_sums(weighted(held, weigh_by_distance(held, dist, spread)), out)


def last_body(held, dist, out, mine, spread):
    weigh = weigh_by_distance(held, dist, spread)
    sums = weighted(held, weigh)
    deep = out.shape[0] // HALF
    odd = (lax.axis_index("pair") + lax.axis_index("far") // 2) % 2 == 1
    for t in range(deep):
        rows = sums[min(t, len(sums) - 1)]
        for g in range(HALF):
            one, other = (z // 2 for z in (FAR_FIRST[0][g], FAR_FIRST[1][g]))
            out[pl.ds(g * deep + t, 1), :] = jnp.where(odd, rows[other : other + 1], rows[one : one + 1])
    mine[...] = weigh(place(*(lax.axis_index(a) for a in PLANE)))


def distance_body(held, sums, out, rows):
    plane, tiles = held.shape[0], held.shape[1] - 1
    whole = [functools.reduce(jnp.add, [sums[g, t] for g in range(sums.shape[0])]) for t in range(tiles // 2 + 1)]
    top = sublane() < HALF
    median = []
    for t in range(tiles // 2):
        m = whole[t] / whole[tiles // 2]
        r = pltpu.roll(m, HALF, 0)
        median += [jnp.where(top, m, r), jnp.where(top, r, m)]

    def step(src, carry):
        acc = None
        for t in range(tiles):
            diff = held[src, t] - median[t]
            acc = diff * diff if acc is None else acc + diff * diff
        rows[pl.ds(pl.multiple_of(src * SUB, SUB), SUB), :] = acc
        return carry

    lax.fori_loop(0, plane, step, 0, unroll=8)
    clients = 2 * plane
    lanes = []
    for g in range(clients // SUB):
        parts = [rows[pl.ds(g * SUB * HALF + i, SUB, stride=HALF), :] for i in range(HALF)]
        lanes.append(functools.reduce(jnp.add, parts))
    lanes = jnp.concatenate(lanes + [jnp.zeros((LANES - clients, LANES), jnp.float32)], axis=0)
    out[...] = jnp.sum(lanes.T, axis=0, keepdims=True)


def finish_body(total_clients, got, mine, median, shares):
    tiles = median.shape[1] // LANES
    whole = functools.reduce(jnp.add, [got[g] for g in range(got.shape[0])])
    total = whole[tiles : tiles + 1]
    part = whole / total
    for t in range(tiles):
        median[:, pl.ds(t * LANES, LANES)] = part[t : t + 1]
    share = total_clients * mine[...] / total
    lane = lax.broadcasted_iota(jnp.int32, (1, LANES), 1)
    share = jnp.where(lane == 0, share[:1], share[HALF : HALF + 1])
    shares[...] = share[0, : shares.shape[0]]


def along_z(value):
    return lax.all_to_all(value, LINE, 0, 0, tiled=True, axis_index_groups=FAR_FIRST)


def local(updates, sample_counts):
    clients, rows, columns = updates.shape
    ny, nfar, npair, nx = (lax.axis_size(a) for a in CLIENT)
    plane = ny * npair * nx
    tiles = columns // LANES
    deep = 2 * SUB

    updates = updates.reshape(clients, rows // SUB, SUB, tiles, LANES).transpose(0, 1, 3, 2, 4)
    updates = updates.reshape(clients, ny, rows // ny * tiles, LANES)
    held = call(
        functools.partial(pack_body, tiles),
        f32(plane, tiles + 1, SUB, LANES),
        [HBM, HBM],
        "pack",
        scratch=[
            pltpu.VMEM((ny, clients * (rows // ny) * tiles, LANES), jnp.float32),
            pltpu.SMEM((clients,), jnp.int32),
            pltpu.SemaphoreType.DMA((clients, ny)),
            pltpu.SemaphoreType.DMA,
        ],
    )(*(pltpu.with_memory_space_constraint(a, pltpu.HBM) for a in (updates, sample_counts)))
    held = lax.all_to_all(held, CLIENT, 0, 0, tiled=True, axis_index_groups=planes())

    per_row = [pltpu.VMEM((plane * SUB, LANES), jnp.float32)]
    payload = f32(nfar, tiles // 2 + 1, SUB, LANES)
    sums = call(start_body, payload, [VMEM], "start")(held)
    for iteration in range(ITERS):
        dist = call(distance_body, f32(1, LANES), [VMEM, VMEM], "distance", scratch=per_row)(held, along_z(sums))
        dist = jnp.broadcast_to(dist[None], (plane * lax.axis_size("param"), 1, LANES))
        dist = lax.all_to_all(dist, PLANE_CORES, 0, 0, tiled=True)
        if iteration < ITERS - 1:
            sums = call(again_body, payload, [VMEM, VMEM], "again", scratch=per_row)(held, dist)
    last, mine = call(
        last_body, (f32(nfar * deep, LANES), f32(SUB, LANES)), [VMEM, VMEM], "last", scratch=per_row
    )(held, dist)
    median, shares = call(
        functools.partial(finish_body, clients * plane * nfar), (f32(1, columns), f32(clients)), [VMEM, VMEM], "finish"
    )(along_z(last.reshape(nfar, deep, LANES)), mine)
    return median, shares


def solution(mesh):
    finer = Mesh(
        mesh.devices.reshape(4, 4, 2, 4, mesh.shape["param"]),
        ("y", "far", "pair", "x", "param"),
    )
    return jax.shard_map(
        local,
        mesh=finer,
        in_specs=(P(CLIENT, None, "param"), P(CLIENT)),
        out_specs=(P(CLIENT, "param"), P(CLIENT)),
        check_vma=False,
    )
```

```python
import functools

import jax
import jax.numpy as jnp
from jax import lax
from jax.experimental import pallas as pl
from jax.experimental.pallas import tpu as pltpu
from jax.sharding import Mesh
from jax.sharding import PartitionSpec as P

ITERS = 2
SMOOTHING = 1e-06

CLIENT = ("y", "far", "pair", "x")
PLANE = ("y", "pair", "x")
PLANE_CORES = ("y", "pair", "x", "param")
LINE = ("far", "pair")
FAR_FIRST = ((0, 5, 2, 7), (4, 1, 6, 3))


def place(y, pair, x):
    return (pair + x) % 2 * 16 + (y + 4 - x) % 4 * 4 + x


def planes():
    order = sorted((place(y, p, x), y, p, x) for y in range(4) for p in range(2) for x in range(4))
    return tuple(tuple(((y * 4 + f) * 2 + p) * 4 + x for _, y, p, x in order) for f in range(4))


SUB = 8
HALF = SUB // 2
LANES = 128
VMEM = pl.BlockSpec(memory_space=pltpu.VMEM)
HBM = pl.BlockSpec(memory_space=pltpu.HBM)


def call(body, outs, in_specs, name, scratch=()):
    return pl.pallas_call(
        body,
        out_shape=outs,
        in_specs=in_specs,
        out_specs=jax.tree.map(lambda _: VMEM, outs),
        scratch_shapes=scratch,
        compiler_params=pltpu.CompilerParams(vmem_limit_bytes=8 << 20),
        name=name,
    )


def f32(*shape):
    return jax.ShapeDtypeStruct(shape, jnp.float32)


def sublane():
    return lax.broadcasted_iota(jnp.int32, (SUB, LANES), 0)


def pack_body(tiles, u_hbm, counts_hbm, out, buf, counts, sems, counts_sem):
    clients, ny, span, _ = u_hbm.shape
    step = tiles * SUB
    nx = HALF

    def copy(k, y):
        return pltpu.make_async_copy(u_hbm.at[k, y], buf.at[y, pl.ds(k * span, span), :], sems.at[k, y])

    fetch = pltpu.make_async_copy(counts_hbm, counts, counts_sem)
    fetch.start()
    for y in range(ny):
        for k in range(clients):
            copy(k, y).start()
    row = sublane()
    flip = (lax.axis_index("far") >= 2).astype(jnp.int32)
    mask = ((row >> 1) & 1) == flip
    fetch.wait()
    tile = jnp.where(row < HALF, counts[0], counts[1]).astype(jnp.float32)
    for p in range(out.shape[0]):
        out[p, tiles] = tile
    for y in range(ny):
        for k in range(clients):
            copy(k, y).wait()
        for x in range(nx):
            for t in range(tiles):
                even = buf[y, pl.ds(t * SUB + x, SUB, stride=step), :]
                odd = buf[y, pl.ds(t * SUB + nx + x, SUB, stride=step), :]
                out[place(y, 0, x), t] = jnp.where(mask, even, odd)
                out[place(y, 1, x), t] = jnp.where(mask, odd, even)


def weighted(held, weigh):
    plane, tiles = held.shape[0], held.shape[1] - 1

    def step(src, accs):
        w = weigh(src)
        sums = [accs[t] + w * held[src, t] for t in range(tiles)]
        return (*sums, accs[tiles] + w)

    zero = jnp.zeros((SUB, LANES), jnp.float32)
    accs = lax.fori_loop(0, plane, step, (zero,) * (tiles + 1), unroll=plane)
    return [a + pltpu.roll(a, HALF, 0) for a in accs]


def weigh_by_count(held):
    return lambda src: held[src, held.shape[1] - 1]


def weigh_by_distance(held, dist, spread):
    clients = 2 * held.shape[0]
    total = jnp.sum(dist[:, 0, :], axis=0, keepdims=True)
    column = jnp.broadcast_to(total, (LANES, LANES)).T[:clients]
    for i in range(HALF):
        spread[pl.ds(i, clients, stride=HALF), :] = column
    counts = weigh_by_count(held)

    def weigh(src):
        at = pl.ds(pl.multiple_of(src * SUB, SUB), SUB)
        return counts(src) / jnp.sqrt(spread[at, :] + SMOOTHING)

    return weigh


def give_sums(sums, out):
    top = sublane() < HALF
    tiles = len(sums) - 1
    for g in range(out.shape[0]):
        for t in range(tiles // 2):
            out[g, t] = jnp.where(top, sums[2 * t], sums[2 * t + 1])
        out[g, tiles // 2] = sums[tiles]


def start_body(held, out):
    give_sums(weighted(held, weigh_by_count(held)), out)


def again_body(held, dist, out, spread):
    give_sums(weighted(held, weigh_by_distance(held, dist, spread)), out)


def last_body(held, dist, out, mine, spread):
    weigh = weigh_by_distance(held, dist, spread)
    sums = weighted(held, weigh)
    deep = out.shape[0] // HALF
    odd = (lax.axis_index("pair") + lax.axis_index("far") // 2) % 2 == 1
    for t in range(deep):
        rows = sums[min(t, len(sums) - 1)]
        for g in range(HALF):
            one, other = (z // 2 for z in (FAR_FIRST[0][g], FAR_FIRST[1][g]))
            out[pl.ds(g * deep + t, 1), :] = jnp.where(odd, rows[other : other + 1], rows[one : one + 1])
    mine[...] = weigh(place(*(lax.axis_index(a) for a in PLANE)))


def distance_body(held, sums, out, rows):
    plane, tiles = held.shape[0], held.shape[1] - 1
    whole = [functools.reduce(jnp.add, [sums[g, t] for g in range(sums.shape[0])]) for t in range(tiles // 2 + 1)]
    top = sublane() < HALF
    median = []
    for t in range(tiles // 2):
        m = whole[t] / whole[tiles // 2]
        r = pltpu.roll(m, HALF, 0)
        median += [jnp.where(top, m, r), jnp.where(top, r, m)]

    def step(src, carry):
        acc = None
        for t in range(tiles):
            diff = held[src, t] - median[t]
            acc = diff * diff if acc is None else acc + diff * diff
        rows[pl.ds(pl.multiple_of(src * SUB, SUB), SUB), :] = acc
        return carry

    lax.fori_loop(0, plane, step, 0, unroll=plane)
    clients = 2 * plane
    lanes = []
    for g in range(clients // SUB):
        parts = [rows[pl.ds(g * SUB * HALF + i, SUB, stride=HALF), :] for i in range(HALF)]
        lanes.append(functools.reduce(jnp.add, parts))
    lanes = jnp.concatenate(lanes + [jnp.zeros((LANES - clients, LANES), jnp.float32)], axis=0)
    out[...] = jnp.sum(lanes.T, axis=0, keepdims=True)


def finish_body(total_clients, got, mine, median, shares):
    tiles = median.shape[1] // LANES
    whole = functools.reduce(jnp.add, [got[g] for g in range(got.shape[0])])
    total = whole[tiles : tiles + 1]
    part = whole / total
    for t in range(tiles):
        median[:, pl.ds(t * LANES, LANES)] = part[t : t + 1]
    share = total_clients * mine[...] / total
    lane = lax.broadcasted_iota(jnp.int32, (1, LANES), 1)
    share = jnp.where(lane == 0, share[:1], share[HALF : HALF + 1])
    shares[...] = share[0, : shares.shape[0]]


def along_z(value):
    return lax.all_to_all(value, LINE, 0, 0, tiled=True, axis_index_groups=FAR_FIRST)


def local(updates, sample_counts):
    clients, rows, columns = updates.shape
    ny, nfar, npair, nx = (lax.axis_size(a) for a in CLIENT)
    plane = ny * npair * nx
    tiles = columns // LANES
    deep = 2 * SUB

    updates = updates.reshape(clients, rows // SUB, SUB, tiles, LANES).transpose(0, 1, 3, 2, 4)
    updates = updates.reshape(clients, ny, rows // ny * tiles, LANES)
    held = call(
        functools.partial(pack_body, tiles),
        f32(plane, tiles + 1, SUB, LANES),
        [HBM, HBM],
        "pack",
        scratch=[
            pltpu.VMEM((ny, clients * (rows // ny) * tiles, LANES), jnp.float32),
            pltpu.SMEM((clients,), jnp.int32),
            pltpu.SemaphoreType.DMA((clients, ny)),
            pltpu.SemaphoreType.DMA,
        ],
    )(*(pltpu.with_memory_space_constraint(a, pltpu.HBM) for a in (updates, sample_counts)))
    held = lax.all_to_all(held, CLIENT, 0, 0, tiled=True, axis_index_groups=planes())

    per_row = [pltpu.VMEM((plane * SUB, LANES), jnp.float32)]
    payload = f32(nfar, tiles // 2 + 1, SUB, LANES)
    sums = call(start_body, payload, [VMEM], "start")(held)
    for iteration in range(ITERS):
        dist = call(distance_body, f32(1, LANES), [VMEM, VMEM], "distance", scratch=per_row)(held, along_z(sums))
        dist = jnp.broadcast_to(dist[None], (plane * lax.axis_size("param"), 1, LANES))
        dist = lax.all_to_all(dist, PLANE_CORES, 0, 0, tiled=True)
        if iteration < ITERS - 1:
            sums = call(again_body, payload, [VMEM, VMEM], "again", scratch=per_row)(held, dist)
    last, mine = call(
        last_body, (f32(nfar * deep, LANES), f32(SUB, LANES)), [VMEM, VMEM], "last", scratch=per_row
    )(held, dist)
    median, shares = call(
        functools.partial(finish_body, clients * plane * nfar), (f32(1, columns), f32(clients)), [VMEM, VMEM], "finish"
    )(along_z(last.reshape(nfar, deep, LANES)), mine)
    return median, shares


def solution(mesh):
    finer = Mesh(
        mesh.devices.reshape(4, 4, 2, 4, mesh.shape["param"]),
        ("y", "far", "pair", "x", "param"),
    )
    return jax.shard_map(
        local,
        mesh=finer,
        in_specs=(P(CLIENT, None, "param"), P(CLIENT)),
        out_specs=(P(CLIENT, "param"), P(CLIENT)),
        check_vma=False,
    )
```
